32 devices in a mesh: batch: 2 (over x), seq: 16 (over z, y, core).
Axes of the slice: x: 2, y: 2, z: 4, core: 2. Of those that a mesh axis runs over, the one named last changes fastest.
Arguments:
- tokens: bfloat16 [2, 4096, 1024], P('batch', 'seq'), may hold values from -6 to 6
- ln1_gain: float32 [1024], replicated, may hold values from 0.5 to 1.5
- ln1_bias: float32 [1024], replicated, may hold values from -3 to 3
- w_qkv: bfloat16 [1024, 3072], replicated, may hold values from -0.1875 to 0.1875
- w_out: bfloat16 [1024, 1024], replicated, may hold values from -6 to 6
- ln2_gain: float32 [1024], replicated, may hold values from 0.5 to 1.5
- ln2_bias: float32 [1024], replicated, may hold values from -3 to 3
- w_up: bfloat16 [1024, 4096], replicated, may hold values from -0.1875 to 0.1875
- w_down: bfloat16 [4096, 1024], replicated, may hold values from -0.09375 to 0.09375
- cotangent: bfloat16 [2, 4096, 1024], P('batch', 'seq'), may hold values from -6 to 6
Outputs:
- output: bfloat16 [2, 4096, 1024], P('batch', 'seq')
- input_grad: bfloat16 [2, 4096, 1024], P('batch', 'seq')
- grad_ln1_gain: float32 [1024], P(('batch', 'seq'))
- grad_ln1_bias: float32 [1024], P(('batch', 'seq'))
- grad_w_qkv: float32 [1024, 3072], P(('batch', 'seq'))
- grad_w_out: float32 [1024, 1024], P(('batch', 'seq'))
- grad_ln2_gain: float32 [1024], P(('batch', 'seq'))
- grad_ln2_bias: float32 [1024], P(('batch', 'seq'))
- grad_w_up: float32 [1024, 4096], P(('batch', 'seq'))
- grad_w_down: float32 [4096, 1024], P(('batch', 'seq'))
The draws below stay inside these ranges and needn't reach their ends.
All inputs are finite; a program needn't handle non-finite values.
Results may differ from the reference program's by a relative error of at most 0.017.
Values may be sent and summed in bfloat16 or wider, within the bound.
No kernel may reach another device: no remote copies, remote signals or barrier semaphores. Data moves between devices by JAX's collectives and lax.ppermute only.
A program may use at most 384 MiB of HBM per device.

```python
import math
import jax
import jax.numpy as jnp
from jax import lax

D = 1024
HEADS = 16
HEAD_DIM = 64
FF = 4096
SCENE_TOK = 4096
SCENES = 2
N_BATCH = 2


def levels(key, dims, shards, least, top_value):
    def one(position, parts):
        steps = jax.random.uniform(jax.random.fold_in(jax.random.fold_in(key, 6), position), (parts,), jnp.float32, least / len(shards), top_value / len(shards))
        return jnp.repeat(jnp.exp(steps), dims[position] // parts).reshape((-1,) + (1,) * (len(dims) - position - 1))

    level = one(*shards[0])
    for cut in shards[1:]:
        level = level * one(*cut)
    return level


def gaussian(own_key, dims, scale, bound, pieces=(), kind=jnp.bfloat16):
    level = levels(own_key, dims, pieces, -0.22, 0.18) if pieces else 1.0
    array = jax.random.normal(own_key, dims, jnp.float32) * scale * level
    return jnp.minimum(jnp.maximum(array, -bound), bound).astype(kind)


def setup_inputs(seed: int = 0) -> dict:
    seeds = jax.random.split(jax.random.key(seed), 11)
    return {
        "tokens": gaussian(seeds[0], (SCENES, SCENE_TOK, D), 1.0, 6.0, ((0, 2), (1, 16))),
        "ln1_gain": jnp.clip(1.0 + 0.1 * jax.random.normal(seeds[1], (D,), jnp.float32), 0.5, 1.5),
        "ln1_bias": gaussian(seeds[2], (D,), 0.5, 3.0, (), jnp.float32),
        "w_qkv": gaussian(seeds[3], (D, 3 * D), D ** -0.5, 0.1875),
        "w_out": gaussian(seeds[4], (D, D), 1 ** -0.5, 6.0),
        "ln2_gain": jnp.clip(1.0 + 0.1 * jax.random.normal(seeds[5], (D,), jnp.float32), 0.5, 1.5),
        "ln2_bias": gaussian(seeds[6], (D,), 0.5, 3.0, (), jnp.float32),
        "w_up": gaussian(seeds[7], (D, FF), D ** -0.5, 0.1875),
        "w_down": gaussian(seeds[8], (FF, D), FF ** -0.5, 0.09375),
        "cotangent": gaussian(seeds[9], (SCENES, SCENE_TOK, D), 1.0, 6.0, ((0, 2), (1, 16))),
    }


@jax.custom_vjp
def low(v):
    return lax.optimization_barrier(v.astype(jnp.bfloat16)).astype(jnp.float32)

@jax.custom_vjp
def low_back(v):
    return v

def low_keep(v):
    return (low(v), None)

def low_pass(kept, grad):
    return (grad,)

def back_keep(v):
    return (v, None)

def back_low(kept, grad):
    return (low(grad),)
low.defvjp(low_keep, low_pass)
low_back.defvjp(back_keep, back_low)
epsilon = 1e-05

def matmul(left, right):
    return jnp.dot(left, right, precision=lax.Precision.HIGHEST, preferred_element_type=jnp.float32)

def layer_norm(values, gain, bias):
    centred = values - lax.optimization_barrier(jnp.mean(values, axis=-1, keepdims=True))
    variance = lax.optimization_barrier(jnp.mean(centred * centred, axis=-1, keepdims=True))
    return centred * lax.rsqrt(variance + epsilon) * gain + bias

def attention(query, keys, values):
    length = query.shape[0]
    block = math.gcd(512, length)
    key_heads = keys.reshape(length, HEADS, HEAD_DIM)
    value_heads = values.reshape(length, HEADS, HEAD_DIM)
    query_blocks = query.reshape(length // block, block, HEADS, HEAD_DIM)

    def one_block(query_block):
        scores = jnp.einsum('qhd,khd->hqk', query_block, key_heads, precision=lax.Precision.HIGHEST) * HEAD_DIM ** (-0.5)
        scores = low_back(scores)
        weights = low(jax.nn.softmax(scores, axis=-1))
        mixed = jnp.einsum('hqk,khd->qhd', weights, value_heads, precision=lax.Precision.HIGHEST)
        return mixed.reshape(block, HEADS * HEAD_DIM)
    result = lax.map(jax.checkpoint(one_block), query_blocks)
    return result.reshape(length, HEADS * HEAD_DIM)

def scene_layer(inputs, ln1_gain, ln1_bias, w_qkv, w_out, ln2_gain, ln2_bias, w_up, w_down):
    width = inputs.shape[1]
    hidden_one = low(layer_norm(inputs, ln1_gain, ln1_bias))
    projected = low_back(low(matmul(hidden_one, w_qkv)))
    query = projected[:, :width]
    keys = projected[:, width:2 * width]
    values = projected[:, 2 * width:]
    mixed = low_back(low(attention(query, keys, values)))
    branch = low_back(matmul(mixed, w_out))
    middle = inputs + branch
    hidden_two = low(layer_norm(middle, ln2_gain, ln2_bias))
    upward = low_back(matmul(hidden_two, w_up))
    active = low(jax.nn.gelu(upward, approximate=True))
    mlp_out = low_back(matmul(active, w_down))
    return middle + mlp_out

def full_layer(inputs, ln1_gain, ln1_bias, w_qkv, w_out, ln2_gain, ln2_bias, w_up, w_down):
    results = []
    for scene in range(N_BATCH):
        results.append(scene_layer(inputs[scene], ln1_gain, ln1_bias, w_qkv, w_out, ln2_gain, ln2_bias, w_up, w_down))
    return jnp.stack(results, axis=0)

def reference(tokens, ln1_gain, ln1_bias, w_qkv, w_out, ln2_gain, ln2_bias, w_up, w_down, cotangent):
    operands = (tokens.astype(jnp.float32), ln1_gain.astype(jnp.float32), ln1_bias.astype(jnp.float32), w_qkv.astype(jnp.float32), w_out.astype(jnp.float32), ln2_gain.astype(jnp.float32), ln2_bias.astype(jnp.float32), w_up.astype(jnp.float32), w_down.astype(jnp.float32))
    output, pull = jax.vjp(full_layer, *operands)
    grads = pull(cotangent.astype(jnp.float32))
    return (output.astype(jnp.bfloat16), grads[0].astype(jnp.bfloat16), grads[1], grads[2], grads[3], grads[4], grads[5], grads[6], grads[7], grads[8])
```

```python
import functools

import jax
import jax.numpy as jnp
from jax import lax
from jax.experimental import pallas as pl
from jax.experimental.pallas import tpu as pltpu
from jax.sharding import PartitionSpec as P

HEADS = 16
EPS = 1e-05
LOG2E = 1.4426950408889634
F32 = jnp.float32
BF16 = jnp.bfloat16


def dot(a, b, ca, cb, kind=F32):
    out = lax.dot_general(a, b, (((ca,), (cb,)), ((), ())), preferred_element_type=F32)
    return out.astype(kind)


def forward_kernel(qb, kc, unroll, q_ref, k_ref, v_ref, o_ref, low_ref, lse_ref, kn, vt):
    sources, _, _, dh, t = k_ref.shape

    @pl.when(pl.program_id(1) == 0)
    def _():
        for i in range(sources):
            kn[i * t : (i + 1) * t, :] = k_ref[i, 0, 0].T
            vt[:, i * t : (i + 1) * t] = v_ref[i, 0, 0]

    q = jnp.concatenate([q_ref[i, 0, 0] for i in range(qb)], axis=1) * BF16(dh**-0.5)

    def step(j, carry):
        top, total, acc = carry
        keys = pl.ds(pl.multiple_of(j * kc, kc), kc)
        s = jnp.dot(kn[keys, :], q, preferred_element_type=F32) * LOG2E
        new_top = jnp.maximum(top, jnp.max(s, axis=0, keepdims=True))
        fix = jnp.exp2(top - new_top)
        p = jnp.exp2(s - new_top)
        total = total * fix + jnp.sum(p, axis=0, keepdims=True)
        acc = acc * fix + jnp.dot(vt[:, keys], p.astype(BF16), preferred_element_type=F32)
        return new_top, total, acc

    start = (
        jnp.full((1, qb * t), -1e30, F32),
        jnp.zeros((1, qb * t), F32),
        jnp.zeros((dh, qb * t), F32),
    )
    top, total, acc = lax.fori_loop(0, sources * t // kc, step, start, unroll=unroll)
    o = acc / total
    lse = top + jnp.log2(total)
    for i in range(qb):
        cols = slice(i * t, (i + 1) * t)
        o_ref[i, 0] = o[:, cols]
        low_ref[i, 0] = o[:, cols].astype(BF16)
        lse_ref[i, 0] = lse[:, cols]


def attention_forward(x, kv):
    g, hl, _, dh, t = x.shape
    sources = kv.shape[0]
    qb = min(4, g)
    kc = min(512, sources * t)
    per_q = lambda d: pl.BlockSpec((qb, 1, d, t), lambda h, i: (i, h, 0, 0))
    part = lambda w: pl.BlockSpec((sources, 1, 1, dh, t), lambda h, i: (0, h, w, 0, 0))
    return pl.pallas_call(
        functools.partial(forward_kernel, qb, kc, 4),
        grid=(hl, g // qb),
        in_specs=[
            pl.BlockSpec((qb, 1, 1, dh, t), lambda h, i: (i, h, 0, 0, 0)),
            part(1),
            part(2),
        ],
        out_specs=[per_q(dh), per_q(dh), per_q(1)],
        out_shape=[
            jax.ShapeDtypeStruct((g, hl, dh, t), F32),
            jax.ShapeDtypeStruct((g, hl, dh, t), BF16),
            jax.ShapeDtypeStruct((g, hl, 1, t), F32),
        ],
        scratch_shapes=[
            pltpu.VMEM((sources * t, dh), BF16),
            pltpu.VMEM((dh, sources * t), BF16),
        ],
        name="attn_fwd",
    )(x, kv, kv)


def backward_kernel(
    qb, kc, unroll, first_ref, q_ref, k_ref, v_ref, do_ref, o_ref, lse_ref, out_ref,
    kn, vn, kt, dka, dva,
):
    sources, _, _, dh, t = k_ref.shape
    step_q = pl.program_id(1)

    @pl.when(step_q == 0)
    def _():
        for i in range(sources):
            cols = slice(i * t, (i + 1) * t)
            kn[cols, :] = k_ref[i, 0, 0].T
            vn[cols, :] = v_ref[i, 0, 0].T
            kt[:, cols] = k_ref[i, 0, 0]
        dka[...] = jnp.zeros_like(dka)
        dva[...] = jnp.zeros_like(dva)
        out_ref[...] = jnp.zeros_like(out_ref)

    beside = lambda ref: jnp.concatenate([ref[i, 0] for i in range(qb)], axis=1)
    scale = dh**-0.5
    qt = jnp.concatenate([q_ref[i, 0, 0] for i in range(qb)], axis=1) * BF16(scale)
    dot_t = beside(do_ref)
    lse = beside(lse_ref)
    delta = jnp.sum(dot_t.astype(F32) * beside(o_ref), axis=0, keepdims=True)
    qn = qt.T
    don = dot_t.T

    def step(j, dq):
        keys = pl.ds(pl.multiple_of(j * kc, kc), kc)
        s = jnp.dot(kn[keys, :], qt, preferred_element_type=F32) * LOG2E
        p = jnp.exp2(s - lse)
        dp = jnp.dot(vn[keys, :], dot_t, preferred_element_type=F32)
        ds = (p * (dp - delta)).astype(BF16)
        dva[keys, :] += jnp.dot(p.astype(BF16), don, preferred_element_type=F32)
        dka[keys, :] += jnp.dot(ds, qn, preferred_element_type=F32)
        return dq + jnp.dot(kt[:, keys], ds, preferred_element_type=F32)

    count = sources * t // kc
    dq = lax.fori_loop(0, count, step, jnp.zeros((dh, qb * t), F32), unroll=unroll) * scale
    for i in range(qb):
        out_ref[first_ref[0] + step_q * qb + i, 0, 0] = dq[:, i * t : (i + 1) * t].astype(BF16)

    @pl.when(step_q == pl.num_programs(1) - 1)
    def _():
        for i in range(sources):
            rows = slice(i * t, (i + 1) * t)
            out_ref[i, 0, 1] = dka[rows, :].astype(BF16).T
            out_ref[i, 0, 2] = dva[rows, :].astype(BF16).T


def attention_backward(x, kv, do, o, lse, first):
    g, hl, _, dh, t = x.shape
    sources = kv.shape[0]
    qb = min(2, g)
    kc = min(512, sources * t)
    per_q = lambda d: pl.BlockSpec((qb, 1, d, t), lambda h, i, f: (i, h, 0, 0))
    part = lambda w: pl.BlockSpec((sources, 1, 1, dh, t), lambda h, i, f: (0, h, w, 0, 0))
    return pl.pallas_call(
        functools.partial(backward_kernel, qb, kc, 8),
        grid_spec=pltpu.PrefetchScalarGridSpec(
            num_scalar_prefetch=1,
            grid=(hl, g // qb),
            in_specs=[
                pl.BlockSpec((qb, 1, 1, dh, t), lambda h, i, f: (i, h, 0, 0, 0)),
                part(1),
                part(2),
                per_q(dh),
                per_q(dh),
                per_q(1),
            ],
            out_specs=pl.BlockSpec((sources, 1, 3, dh, t), lambda h, i, f: (0, h, 0, 0, 0)),
            scratch_shapes=[
                pltpu.VMEM((sources * t, dh), BF16),
                pltpu.VMEM((sources * t, dh), BF16),
                pltpu.VMEM((dh, sources * t), BF16),
                pltpu.VMEM((sources * t, dh), F32),
                pltpu.VMEM((sources * t, dh), F32),
            ],
        ),
        out_shape=jax.ShapeDtypeStruct((sources, hl, 3, dh, t), BF16),
        name="attn_bwd",
    )(first, x, kv, kv, do, o, lse)


def log2(size):
    bits = size.bit_length() - 1
    assert 1 << bits == size
    return bits


def swap(value, bit):
    axis, amount = bit
    size = lax.axis_size(axis)
    return lax.ppermute(value, axis, [(i, i ^ amount) for i in range(size)])


def place_of_bits():
    seq_bits = [("seq", 1 << i) for i in range(log2(lax.axis_size("seq")))]
    batch_bits = [("batch", 1 << i) for i in range(log2(lax.axis_size("batch")))]
    return [seq_bits[0]] + batch_bits[::-1] + seq_bits[:0:-1], batch_bits, seq_bits


def owner_of_position(bits):
    size = lax.axis_size("seq")
    position = jnp.arange(1 << len(bits))
    other = jnp.zeros_like(position)
    for i, (axis, amount) in enumerate(reversed(bits)):
        weight = amount if axis == "seq" else amount * size
        other = other + ((position >> i) & 1) * weight
    me = lax.axis_index("batch") * size + lax.axis_index("seq")
    return other ^ me


def link_orders():
    _, batch_bits, seq_bits = place_of_bits()
    first = [batch_bits[:1], seq_bits[1:2], seq_bits[2:3]]
    rest = batch_bits[1:] + seq_bits[3:]
    flat = lambda k: [b for i in range(3) for b in first[(k + i) % 3]] + rest
    return [flat(0), flat(1), flat(2)]


def reduce_chunk(send, keep, order, bits):
    got = swap(send, bits[0])
    left = list(bits[1:])
    shape = (2,) * len(left) + keep.shape[1:]
    got, keep = got.reshape(shape), keep.reshape(shape)
    for bit in order:
        axis = left.index(bit)
        take = lambda v, k: lax.index_in_dim(v, k, axis, keepdims=False)
        half = lambda k: (take(got, k).astype(F32) + take(keep, k).astype(F32)).astype(BF16)
        got, keep = swap(half(1), bit), half(0)
        left.remove(bit)
    return got.astype(F32) + keep.astype(F32)


def normalize(values, gain, bias):
    centred = values - jnp.mean(values, axis=-1, keepdims=True)
    variance = jnp.mean(centred * centred, axis=-1, keepdims=True)
    inv_root = lax.rsqrt(variance + EPS)
    normed = centred * inv_root
    return (normed * gain + bias, normed, inv_root)


def norm_back(grad_out, normed, inv_root, gain):
    grad_normed = grad_out * gain
    grad_in = inv_root * (
        grad_normed
        - jnp.mean(grad_normed, axis=-1, keepdims=True)
        - normed * jnp.mean(grad_normed * normed, axis=-1, keepdims=True)
    )
    return (grad_in, jnp.sum(grad_out * normed, axis=0), jnp.sum(grad_out, axis=0))


def permute_kernel(blocks, own_ref, a_ref, o_ref):
    width = a_ref.shape[1] // blocks
    for j in range(blocks):
        start = pl.multiple_of(own_ref[j] * width, width)
        o_ref[:, j * width : (j + 1) * width] = a_ref[:, pl.ds(start, width)]


def permute_blocks(a, owners):
    blocks = owners.shape[0]
    if a.shape[1] // blocks % 128:
        return a.reshape(a.shape[0], blocks, -1)[:, owners].reshape(a.shape)
    return pl.pallas_call(
        functools.partial(permute_kernel, blocks),
        grid_spec=pltpu.PrefetchScalarGridSpec(
            num_scalar_prefetch=1,
            grid=(1,),
            in_specs=[pl.BlockSpec(a.shape, lambda i, o: (0, 0))],
            out_specs=pl.BlockSpec(a.shape, lambda i, o: (0, 0)),
        ),
        out_shape=jax.ShapeDtypeStruct(a.shape, a.dtype),
        name="permute_blocks",
    )(owners, a)


def body(tokens, ln1_gain, ln1_bias, w_qkv, w_out, ln2_gain, ln2_bias, w_up, w_down, cotangent):
    x = tokens[0].astype(F32)
    t, d = x.shape
    dh = d // HEADS
    n = lax.axis_size("seq")
    both = ("batch", "seq")
    g = min(n, HEADS)
    hl = HEADS // g
    r = n // g
    near = [[k * g + i for i in range(g)] for k in range(r)] if r > 1 else None
    far = [[k * g + i for k in range(r)] for i in range(g)]
    bits, _, _ = place_of_bits()
    orders = link_orders()
    blocks = 1 << len(bits)
    half = blocks // 2
    owners = owner_of_position(bits).astype(jnp.int32)
    row = jnp.arange(d)
    width = d // blocks
    source = jnp.repeat(owners * width, width) + row % width
    one_hot = (row[:, None] == source[None, :]).astype(BF16)

    exchange = lambda v: lax.all_to_all(v, "seq", 0, 0, axis_index_groups=near, tiled=True)

    hidden, normed_one, root_one = normalize(x, ln1_gain, ln1_bias)
    h1 = hidden.astype(BF16)
    projected = dot(w_qkv, h1, 0, 1, BF16)
    heads = projected.reshape(3, HEADS, dh, t).transpose(1, 0, 2, 3)
    qkv = exchange(heads.reshape(g, hl, 3, dh, t))
    kv = lax.all_gather(qkv, "seq", axis=0, tiled=True, axis_index_groups=far) if r > 1 else qkv
    o, o_low, lse = attention_forward(qkv, kv)
    mixed = exchange(o_low).reshape(d, t)
    middle = x + dot(mixed, w_out, 0, 0)
    hidden2, normed_two, root_two = normalize(middle, ln2_gain, ln2_bias)
    h2 = hidden2.astype(BF16)
    upward = dot(h2, w_up, 1, 0)
    active = jax.nn.gelu(upward, approximate=True).astype(BF16)
    output = (middle + dot(active, w_down, 1, 0)).astype(BF16)[None]

    top = cotangent[0]
    active_p = permute_blocks(active, owners)
    grad_active = dot(top, w_down, 1, 1)
    _, gelu_pull = jax.vjp(lambda v: jax.nn.gelu(v, approximate=True), upward)
    du = gelu_pull(grad_active)[0].astype(BF16)
    h2_p = dot(h2, one_hot, 1, 0, BF16)

    def scatter(rows, columns, order):
        both_halves = [
            dot(part, columns, 0, 0, BF16).reshape(half, -1, columns.shape[1])
            for part in jnp.split(rows, 2, axis=1)
        ]
        return reduce_chunk(both_halves[1], both_halves[0], order, bits)

    def scatter_cols(rows, columns, cuts):
        edges = [0] + [c for c, _ in cuts]
        pieces = [
            scatter(rows, columns[:, edges[i] : edges[i + 1]], orders[cuts[i][1]])
            for i in range(len(cuts))
        ]
        return jnp.concatenate([p.reshape(-1, p.shape[-1]) for p in pieces], axis=1)

    ff = w_up.shape[1]
    cut_d = 2 * d // 3 // 128 * 128
    cut_f = 2 * ff // 3 // 128 * 128
    down_sum = scatter_cols(active_p, top, [(cut_d, 0), (d, 2)])
    up_sum = scatter_cols(h2_p, du, [(cut_f, 1), (ff, 2)])

    grad_h2 = dot(du, w_up, 1, 1)
    grad_part_two, gain_two, bias_two = norm_back(grad_h2, normed_two, root_two, ln2_gain)
    grad_middle = top.astype(F32) + grad_part_two
    dattn = grad_middle.astype(BF16)
    do = dot(w_out, dattn, 1, 1, BF16)
    mixed_p = dot(mixed, one_hot, 0, 0, BF16)
    out_sum = scatter_cols(mixed_p, dattn, [(d, 0)])

    do_heads = exchange(do.reshape(g, hl, dh, t))
    first = jnp.full((1,), lax.axis_index("seq") // g * g if r > 1 else 0, jnp.int32)
    dqkv_heads = attention_backward(qkv, kv, do_heads, o, lse, first)
    if r > 1:
        dqkv_heads = lax.psum_scatter(
            dqkv_heads, "seq", scatter_dimension=0, tiled=True, axis_index_groups=far
        )
    back = exchange(dqkv_heads).reshape(HEADS, 3, dh, t).transpose(1, 0, 2, 3).reshape(3 * d, t)
    h1_p = dot(h1, one_hot, 1, 0, BF16)
    qkv_sum = scatter_cols(h1_p, back.T, [(d, 0), (2 * d, 1), (3 * d, 2)])
    grad_h1 = dot(back, w_qkv, 0, 1)
    grad_part_one, gain_one, bias_one = norm_back(grad_h1, normed_one, root_one, ln1_gain)
    input_grad = (grad_middle + grad_part_one).astype(BF16)[None]
    small = jnp.stack([gain_one, bias_one, gain_two, bias_two])
    small = small.reshape(4, blocks, -1).transpose(1, 0, 2)
    small = jnp.sum(lax.all_to_all(small, both, 0, 0, tiled=True), axis=0)
    return (
        output, input_grad, small[0], small[1], qkv_sum, out_sum, small[2], small[3], up_sum, down_sum,
    )


def solution(mesh):
    split = P("batch", "seq", None)
    spread = ("batch", "seq")
    return jax.shard_map(
        body,
        mesh=mesh,
        in_specs=(split, P(), P(), P(), P(), P(), P(), P(), P(), split),
        out_specs=(
            split,
            split,
            P(spread),
            P(spread),
            P(spread, None),
            P(spread, None),
            P(spread),
            P(spread),
            P(spread, None),
            P(spread, None),
        ),
        check_vma=False,
    )
```

```python
import functools
import math

import jax
import jax.numpy as jnp
from jax import lax
from jax.experimental import pallas as pl
from jax.experimental.pallas import tpu as pltpu
from jax.sharding import PartitionSpec as P

HEADS = 16
EPS = 1e-05
LOG2E = 1.4426950408889634
F32 = jnp.float32
BF16 = jnp.bfloat16
MESH_AXES = ("batch", "rep", "z", "y", "core")
SEQ = ("rep", "z", "y", "core")
GROUP = ("z", "y", "core")


def dot(a, b, ca, cb, kind=F32):
    out = lax.dot_general(a, b, (((ca,), (cb,)), ((), ())), preferred_element_type=F32)
    return out.astype(kind)


def forward_kernel(qb, kc, unroll, q_ref, k_ref, v_ref, o_ref, low_ref, lse_ref, kn, vt):
    sources, _, _, dh, t = k_ref.shape

    @pl.when(pl.program_id(1) == 0)
    def _():
        for i in range(sources):
            kn[i * t : (i + 1) * t, :] = k_ref[i, 0, 0].T
            vt[:, i * t : (i + 1) * t] = v_ref[i, 0, 0]

    q = jnp.concatenate([q_ref[i, 0, 0] for i in range(qb)], axis=1) * BF16(dh**-0.5)

    def step(j, carry):
        top, total, acc = carry
        keys = pl.ds(pl.multiple_of(j * kc, kc), kc)
        s = jnp.dot(kn[keys, :], q, preferred_element_type=F32) * LOG2E
        new_top = jnp.maximum(top, jnp.max(s, axis=0, keepdims=True))
        fix = jnp.exp2(top - new_top)
        p = jnp.exp2(s - new_top)
        total = total * fix + jnp.sum(p, axis=0, keepdims=True)
        acc = acc * fix + jnp.dot(vt[:, keys], p.astype(BF16), preferred_element_type=F32)
        return new_top, total, acc

    start = (
        jnp.full((1, qb * t), -1e30, F32),
        jnp.zeros((1, qb * t), F32),
        jnp.zeros((dh, qb * t), F32),
    )
    top, total, acc = lax.fori_loop(0, sources * t // kc, step, start, unroll=unroll)
    o = acc / total
    lse = top + jnp.log2(total)
    for i in range(qb):
        cols = slice(i * t, (i + 1) * t)
        o_ref[i, 0] = o[:, cols]
        low_ref[i, 0] = o[:, cols].astype(BF16)
        lse_ref[i, 0] = lse[:, cols]


def attention_forward(x, kv):
    g, hl, _, dh, t = x.shape
    sources = kv.shape[0]
    qb = min(4, g)
    kc = min(512, sources * t)
    per_q = lambda d: pl.BlockSpec((qb, 1, d, t), lambda h, i: (i, h, 0, 0))
    part = lambda w: pl.BlockSpec((sources, 1, 1, dh, t), lambda h, i: (0, h, w, 0, 0))
    return pl.pallas_call(
        functools.partial(forward_kernel, qb, kc, 4),
        grid=(hl, g // qb),
        in_specs=[
            pl.BlockSpec((qb, 1, 1, dh, t), lambda h, i: (i, h, 0, 0, 0)),
            part(1),
            part(2),
        ],
        out_specs=[per_q(dh), per_q(dh), per_q(1)],
        out_shape=[
            jax.ShapeDtypeStruct((g, hl, dh, t), F32),
            jax.ShapeDtypeStruct((g, hl, dh, t), BF16),
            jax.ShapeDtypeStruct((g, hl, 1, t), F32),
        ],
        scratch_shapes=[
            pltpu.VMEM((sources * t, dh), BF16),
            pltpu.VMEM((dh, sources * t), BF16),
        ],
        cost_estimate=pl.CostEstimate(
            flops=16 * dh * g * hl * t * sources * t,
            transcendentals=g * hl * t * sources * t,
            bytes_accessed=16 * g * hl * dh * t,
        ),
        name="attn_fwd",
    )(x, kv, kv)


def backward_kernel(qb, kc, unroll, last, *refs):
    if last:
        first_ref, q_ref, k_ref, v_ref, do_ref, o_ref, lse_ref, dq_in, dkv_in = refs[:9]
        out_ref, kn, vn, kt, dka, dva = refs[9:]
        before = dkv_in.shape[0]
    else:
        _, q_ref, k_ref, v_ref, do_ref, o_ref, lse_ref, dq_out, dkv_out = refs[:9]
        kn, vn, kt, dka, dva = refs[9:]
    sources, _, _, dh, t = k_ref.shape
    step_q = pl.program_id(1)

    @pl.when(step_q == 0)
    def _():
        for i in range(sources):
            cols = slice(i * t, (i + 1) * t)
            kn[cols, :] = k_ref[i, 0, 0].T
            vn[cols, :] = v_ref[i, 0, 0].T
            kt[:, cols] = k_ref[i, 0, 0]
        dka[...] = jnp.zeros_like(dka)
        dva[...] = jnp.zeros_like(dva)
        if last:
            out_ref[:, 0, 0] = jnp.zeros(out_ref.shape[:1] + (dh, t), BF16)
            for i in range(before):
                out_ref[i, 0, 1:3] = dkv_in[i, 0]

    beside = lambda ref: jnp.concatenate([ref[i, 0] for i in range(qb)], axis=1)
    scale = dh**-0.5
    qt = jnp.concatenate([q_ref[i, 0, 0] for i in range(qb)], axis=1) * BF16(scale)
    dot_t = beside(do_ref)
    lse = beside(lse_ref)
    delta = jnp.sum(dot_t.astype(F32) * beside(o_ref), axis=0, keepdims=True)
    qn = qt.T
    don = dot_t.T

    def step(j, dq):
        keys = pl.ds(pl.multiple_of(j * kc, kc), kc)
        s = jnp.dot(kn[keys, :], qt, preferred_element_type=F32) * LOG2E
        p = jnp.exp2(s - lse)
        dp = jnp.dot(vn[keys, :], dot_t, preferred_element_type=F32)
        ds = (p * (dp - delta)).astype(BF16)
        dva[keys, :] += jnp.dot(p.astype(BF16), don, preferred_element_type=F32)
        dka[keys, :] += jnp.dot(ds, qn, preferred_element_type=F32)
        return dq + jnp.dot(kt[:, keys], ds, preferred_element_type=F32)

    count = sources * t // kc
    start = beside(dq_in) if last else jnp.zeros((dh, qb * t), F32)
    dq = lax.fori_loop(0, count, step, start, unroll=min(unroll, count))
    for i in range(qb):
        cols = slice(i * t, (i + 1) * t)
        if last:
            place = first_ref[0] + step_q * qb + i
            out_ref[place, 0, 0] = (dq[:, cols] * scale).astype(BF16)
        else:
            dq_out[i, 0] = dq[:, cols]

    @pl.when(step_q == pl.num_programs(1) - 1)
    def _():
        for i in range(sources):
            rows = slice(i * t, (i + 1) * t)
            if last:
                out_ref[before + i, 0, 1] = dka[rows, :].astype(BF16).T
                out_ref[before + i, 0, 2] = dva[rows, :].astype(BF16).T
            else:
                dkv_out[i, 0, 0] = dka[rows, :].astype(BF16).T
                dkv_out[i, 0, 1] = dva[rows, :].astype(BF16).T


def attention_backward(x, kv, do, o, lse, first, carried=None):
    g, hl, _, dh, t = x.shape
    sources = kv.shape[0]
    half = sources // 2
    last = carried is not None
    qb = min(2, g)
    kc = min(512, half * t)
    per_q = lambda d: pl.BlockSpec((qb, 1, d, t), lambda h, i, f: (i, h, 0, 0))
    part = lambda w: pl.BlockSpec((half, 1, 1, dh, t), lambda h, i, f: (int(last), h, w, 0, 0))
    some = pl.BlockSpec((half, 1, 2, dh, t), lambda h, i, f: (0, h, 0, 0, 0))
    full = pl.BlockSpec((sources, 1, 3, dh, t), lambda h, i, f: (0, h, 0, 0, 0))
    shape = lambda s, k=BF16: jax.ShapeDtypeStruct(s, k)
    pairs = g * hl * t * half * t
    return pl.pallas_call(
        functools.partial(backward_kernel, qb, kc, 8, last),
        grid_spec=pltpu.PrefetchScalarGridSpec(
            num_scalar_prefetch=1,
            grid=(hl, g // qb),
            in_specs=[
                pl.BlockSpec((qb, 1, 1, dh, t), lambda h, i, f: (i, h, 0, 0, 0)),
                part(1),
                part(2),
                per_q(dh),
                per_q(dh),
                per_q(1),
            ]
            + ([per_q(dh), some] if last else []),
            out_specs=full if last else [per_q(dh), some],
            scratch_shapes=[
                pltpu.VMEM((half * t, dh), BF16),
                pltpu.VMEM((half * t, dh), BF16),
                pltpu.VMEM((dh, half * t), BF16),
                pltpu.VMEM((half * t, dh), F32),
                pltpu.VMEM((half * t, dh), F32),
            ],
        ),
        out_shape=shape((sources, hl, 3, dh, t))
        if last
        else [shape((g, hl, dh, t), F32), shape((half, hl, 2, dh, t))],
        cost_estimate=pl.CostEstimate(
            flops=40 * dh * pairs, transcendentals=pairs, bytes_accessed=8 * g * hl * dh * t * 2
        ),
        name="attn_bwd",
    )(first, x, kv, kv, do, o, lse, *(carried or ()))


def normalize(values, gain, bias):
    centred = values - jnp.mean(values, axis=-1, keepdims=True)
    variance = jnp.mean(centred * centred, axis=-1, keepdims=True)
    inv_root = lax.rsqrt(variance + EPS)
    normed = centred * inv_root
    return (normed * gain + bias, normed, inv_root)


def norm_back(grad_out, normed, inv_root, gain):
    grad_normed = grad_out * gain
    grad_in = inv_root * (
        grad_normed
        - jnp.mean(grad_normed, axis=-1, keepdims=True)
        - normed * jnp.mean(grad_normed * normed, axis=-1, keepdims=True)
    )
    gain_sum = jnp.sum(grad_out * normed, axis=0, keepdims=True)
    return (grad_in, gain_sum, jnp.sum(grad_out, axis=0, keepdims=True))


def gelu_and_slope(z):
    k = math.sqrt(2.0 / math.pi)
    square = z * z
    th = jnp.tanh(k * z * (1.0 + 0.044715 * square))
    value = 0.5 * z * (1.0 + th)
    slope = 0.5 * (1.0 + th) + 0.5 * z * (1.0 - th * th) * (k * (1.0 + 3 * 0.044715 * square))
    return value, slope


def whole(shape):
    return pl.BlockSpec(shape, lambda *i: (0,) * len(shape))


def project_kernel(x_ref, gain_ref, bias_ref, wq_ref, wk_ref, wv_ref, h_ref, out_ref, h1):
    @pl.when(pl.program_id(0) == 0)
    def _():
        hidden, _, _ = normalize(x_ref[...].astype(F32), gain_ref[...], bias_ref[...])
        h1[...] = hidden.astype(BF16)
        h_ref[...] = h1[...]

    heads, _, dh, t = out_ref.shape
    for i, w_ref in enumerate((wq_ref, wk_ref, wv_ref)):
        part = dot(h1[...], w_ref[...], 1, 0, BF16)
        out_ref[:, i] = part.T.reshape(heads, dh, t)


def project(x, gain, bias, w_qkv):
    t, d = x.shape
    dh = d // HEADS
    steps = 4
    cols = d // steps
    w_part = lambda k: pl.BlockSpec((d, cols), lambda i: (0, k * steps + i))
    return pl.pallas_call(
        project_kernel,
        grid=(steps,),
        in_specs=[whole((t, d)), whole((1, d)), whole((1, d)), w_part(0), w_part(1), w_part(2)],
        out_specs=[
            whole((t, d)),
            pl.BlockSpec((HEADS // steps, 3, dh, t), lambda i: (i, 0, 0, 0)),
        ],
        out_shape=[
            jax.ShapeDtypeStruct((t, d), BF16),
            jax.ShapeDtypeStruct((HEADS, 3, dh, t), BF16),
        ],
        scratch_shapes=[pltpu.VMEM((t, d), BF16)],
        name="project",
    )(x, gain, bias, w_qkv, w_qkv, w_qkv)


def middle_kernel(
    me_ref, x_ref, mixed_ref, w_out_ref, gain_ref, bias_ref, rows_d_ref, rows_f_ref, up_ref,
    down_ref, top_ref,
    output_ref, grad_ref, do_ref, small_ref, down_keep, down_send, up_keep, up_send, rest_keep,
    rest_send,
    middle, normed, root, h2, h2_t, y_sum, dh2_sum, hot_f,
):
    step = pl.program_id(0)
    d = x_ref.shape[1]

    def one_hot(rows_ref):
        count = rows_ref.shape[0]
        cols = lax.broadcasted_iota(jnp.int32, (count, count), 1)
        return (rows_ref[...] == cols).astype(F32).astype(BF16)

    @pl.when(step == 0)
    def _():
        mid = x_ref[...].astype(F32) + dot(mixed_ref[...].T, w_out_ref[...], 1, 0)
        middle[...] = mid
        hidden, normed[...], root[...] = normalize(mid, gain_ref[...], bias_ref[...])
        h2[...] = hidden.astype(BF16)
        h2_t[...] = dot(one_hot(rows_d_ref), h2[...], 1, 1, BF16)
        hot_f[...] = one_hot(rows_f_ref)
        y_sum[...] = jnp.zeros_like(y_sum)
        dh2_sum[...] = jnp.zeros_like(dh2_sum)

    value, slope = gelu_and_slope(dot(h2[...], up_ref[...], 1, 0))
    active = value.astype(BF16)
    top = top_ref[...]
    du = (dot(top, down_ref[...], 1, 1) * slope).astype(BF16)
    y_sum[...] += dot(active, down_ref[...], 1, 0)
    dh2_sum[...] += dot(du, up_ref[...], 1, 1)
    active_t = dot(hot_f[...], active, 1, 1, BF16)
    half = active_t.shape[0] // 2
    down_keep[...] = dot(active_t[:half], top, 1, 0, BF16).reshape(down_keep.shape)
    down_send[...] = dot(active_t[half:], top, 1, 0, BF16).reshape(down_send.shape)
    main = pl.num_programs(0) * 3 // 4
    up_both = [
        dot(rows, du, 1, 0, BF16).reshape(up_keep.shape)
        for rows in (h2_t[: d // 2, :], h2_t[d // 2 :, :])
    ]

    @pl.when(step < main)
    def _():
        up_keep[...], up_send[...] = up_both

    cols = du.shape[1]
    for i in range(d // cols):

        @pl.when(step == main + i)
        def _():
            rest_keep[:, 0, :, i * cols : (i + 1) * cols] = up_both[0]
            rest_send[:, 0, :, i * cols : (i + 1) * cols] = up_both[1]

    @pl.when(step == pl.num_programs(0) - 1)
    def _():
        output_ref[...] = (middle[...] + y_sum[...]).astype(BF16)
        part, gain_sum, bias_sum = norm_back(dh2_sum[...], normed[...], root[...], gain_ref[...])
        grad = top.astype(F32) + part
        grad_ref[...] = grad
        small_ref[0:1, :] = gain_sum
        small_ref[1:2, :] = bias_sum
        low = grad.astype(BF16)
        do_ref[...] = dot(w_out_ref[...], low, 1, 1, BF16)
        mixed_p = dot(one_hot(rows_d_ref), mixed_ref[...], 1, 0, BF16)
        rest = rest_keep.shape[:1] + rest_keep.shape[2:]
        rest_keep[:, 1] = dot(mixed_p[: d // 2], low, 1, 0, BF16).reshape(rest)
        rest_send[:, 1] = dot(mixed_p[d // 2 :], low, 1, 0, BF16).reshape(rest)


def middle_part(me, devices, x, mixed, w_out, gain, bias, w_up, w_down, top):
    t, d = x.shape
    ff = w_up.shape[1]
    cols = 512
    chips = devices // 2
    per_d, per_f = d // devices, ff // devices
    owners = cols // per_f

    def source_rows(blocks, width):
        position = jnp.arange(blocks)
        relative = position % (blocks // 2) * 2 + position // (blocks // 2)
        start = (relative ^ (me % blocks)) * width
        return (start[:, None] + jnp.arange(width)).reshape(-1, 1).astype(jnp.int32)

    by_step = pl.BlockSpec(
        (owners // 2, per_f, d), lambda i, m: (i ^ (m[0] // owners), 0, 0)
    )
    assert ff == 4 * d
    main = (ff - d) // cols
    up_step = pl.BlockSpec((chips, per_d, cols), lambda i, m: (0, 0, jnp.minimum(i, main - 1)))
    full_out = whole((chips, 2, per_d, d))
    shape = lambda s, k=BF16: jax.ShapeDtypeStruct(s, k)
    return pl.pallas_call(
        middle_kernel,
        grid_spec=pltpu.PrefetchScalarGridSpec(
            num_scalar_prefetch=1,
            grid=(ff // cols,),
            in_specs=[
                whole((t, d)),
                whole((d, t)),
                whole((d, d)),
                whole((1, d)),
                whole((1, d)),
                whole((d, 1)),
                whole((cols, 1)),
                pl.BlockSpec((d, cols), lambda i, m: (0, i)),
                pl.BlockSpec((cols, d), lambda i, m: (i, 0)),
                whole((t, d)),
            ],
            out_specs=[
                whole((t, d)),
                whole((t, d)),
                whole((d, t)),
                whole((2, d)),
                by_step,
                by_step,
                up_step,
                up_step,
                full_out,
                full_out,
            ],
            scratch_shapes=[
                pltpu.VMEM((t, d), F32),
                pltpu.VMEM((t, d), F32),
                pltpu.VMEM((t, 1), F32),
                pltpu.VMEM((t, d), BF16),
                pltpu.VMEM((d, t), BF16),
                pltpu.VMEM((t, d), F32),
                pltpu.VMEM((t, d), F32),
                pltpu.VMEM((cols, cols), BF16),
            ],
        ),
        out_shape=[
            shape((t, d)),
            shape((t, d), F32),
            shape((d, t)),
            shape((2, d), F32),
            shape((chips, per_f, d)),
            shape((chips, per_f, d)),
            shape((chips, per_d, ff - d)),
            shape((chips, per_d, ff - d)),
            shape((chips, 2, per_d, d)),
            shape((chips, 2, per_d, d)),
        ],
        cost_estimate=pl.CostEstimate(
            flops=16 * t * d * ff, transcendentals=t * ff, bytes_accessed=10 * d * ff
        ),
        name="middle",
    )(
        me.reshape(1), x, mixed, w_out, gain, bias, source_rows(devices, per_d),
        source_rows(owners, per_f), w_up, w_down, top,
    )


def product_kernel(d_ref, h_ref, o_ref, acc):
    step = pl.program_id(1)

    @pl.when(step == 0)
    def _():
        acc[...] = jnp.zeros_like(acc)

    count = h_ref.shape[0]
    parts = [dot(d_ref[i, 0].reshape(acc.shape[0], -1), h_ref[i], 1, 0) for i in range(count)]
    acc[...] += sum(parts[1:], parts[0])

    @pl.when(step == pl.num_programs(1) - 1)
    def _():
        o_ref[0] = acc[...].T.astype(o_ref.dtype)


def head_products(grads, hidden):
    g, hl, _, dh, t = grads.shape
    d = hidden.shape[2]
    count = min(4, g)
    return pl.pallas_call(
        product_kernel,
        grid=(hl, g // count),
        in_specs=[
            pl.BlockSpec((count, 1, 3, dh, t), lambda h, i: (i, h, 0, 0, 0)),
            pl.BlockSpec((count, t, d), lambda h, i: (i, 0, 0)),
        ],
        out_specs=pl.BlockSpec((1, d, 3 * dh), lambda h, i: (h, 0, 0)),
        out_shape=jax.ShapeDtypeStruct((hl, d, 3 * dh), BF16),
        scratch_shapes=[pltpu.VMEM((3 * dh, d), F32)],
        name="head_products",
    )(grads, hidden)


def finish_kernel(back_ref, w_ref, x_ref, gain_ref, bias_ref, grad_ref, out_ref, small_ref, acc):
    step = pl.program_id(0)

    @pl.when(step == 0)
    def _():
        acc[...] = jnp.zeros_like(acc)

    d = w_ref.shape[0]
    acc[...] += dot(back_ref[:, 0].reshape(d, -1).T, w_ref[...], 1, 1)

    @pl.when(step == pl.num_programs(0) - 1)
    def _():
        _, normed, root = normalize(x_ref[...].astype(F32), gain_ref[...], bias_ref[...])
        part, gain_sum, bias_sum = norm_back(acc[...], normed, root, gain_ref[...])
        out_ref[...] = (grad_ref[...] + part).astype(BF16)
        small_ref[0:1, :] = gain_sum
        small_ref[1:2, :] = bias_sum


def finish(back, w_qkv, x, gain, bias, grad):
    t, d = x.shape
    dh = d // HEADS
    return pl.pallas_call(
        finish_kernel,
        grid=(3,),
        in_specs=[
            pl.BlockSpec((HEADS, 1, dh, t), lambda i: (0, i, 0, 0)),
            pl.BlockSpec((d, d), lambda i: (0, i)),
            whole((t, d)),
            whole((1, d)),
            whole((1, d)),
            whole((t, d)),
        ],
        out_specs=[whole((t, d)), whole((2, d))],
        out_shape=[jax.ShapeDtypeStruct((t, d), BF16), jax.ShapeDtypeStruct((2, d), F32)],
        scratch_shapes=[pltpu.VMEM((t, d), F32)],
        name="finish",
    )(back, w_qkv, x, gain, bias, grad)


def link_bits():
    bits = []
    for axis in MESH_AXES[:-1]:
        size = lax.axis_size(axis)
        bits += [(axis, size >> (i + 1)) for i in range(size.bit_length() - 1)]
    return bits


def swap(value, bit):
    axis, amount = bit
    size = lax.axis_size(axis)
    return lax.ppermute(value, axis, [(i, i ^ amount) for i in range(size)])


def halving(send, keep, order):
    got = swap(send, ("core", 1))
    left = link_bits()
    shape = (2,) * len(left) + keep.shape[1:]
    got, keep = got.reshape(shape), keep.reshape(shape)
    for bit in order:
        axis = left.index(bit)
        take = lambda v, k: lax.index_in_dim(v, k, axis, keepdims=False)
        half = lambda k: (take(got, k).astype(F32) + take(keep, k).astype(F32)).astype(BF16)
        away, keep = half(1), half(0)
        got = swap(away, bit)
        left.remove(bit)
    return got.astype(F32) + keep.astype(F32)


def body(tokens, ln1_gain, ln1_bias, w_qkv, w_out, ln2_gain, ln2_bias, w_up, w_down, cotangent):
    x = tokens[0]
    t, d = x.shape
    dh = d // HEADS
    g = lax.axis_size(GROUP)
    hl = HEADS // g
    r = lax.axis_size("rep")
    devices = lax.axis_size(MESH_AXES)
    width = d // devices
    me = lax.axis_index(MESH_AXES).astype(jnp.int32)
    row = lambda v: v.reshape(1, d)
    exchange = lambda v: lax.all_to_all(v, GROUP, 0, 0, tiled=True)

    h1, heads = project(x, row(ln1_gain), row(ln1_bias), w_qkv)
    qkv = exchange(heads.reshape(g, hl, 3, dh, t))
    h1_late, qkv = lax.optimization_barrier((h1, qkv))
    h1_all = lax.all_gather(h1_late, GROUP)
    kv = lax.all_gather(qkv, "rep", axis=0, tiled=True) if r > 1 else qkv
    o, o_low, lse = attention_forward(qkv, kv)
    mixed = exchange(o_low).reshape(d, t)
    (
        output, grad_middle, do, small_two, down_keep, down_send, up_keep, up_send, rest_keep, rest_send,
    ) = middle_part(
        me, devices, x, mixed, w_out, row(ln2_gain), row(ln2_bias), w_up, w_down, cotangent[0]
    )

    bits = link_bits()
    batch_bits = [b for b in bits if b[0] == "batch"][::-1]
    y_bits = [b for b in bits if b[0] == "y"]
    z_bits = [b for b in bits if b[0] in ("rep", "z")][::-1]
    down_sum = halving(down_send, down_keep, batch_bits + y_bits + z_bits)
    up_sum = halving(up_send, up_keep, y_bits + batch_bits + z_bits)
    rest_sum = halving(rest_send, rest_keep, z_bits + batch_bits + y_bits)
    up_sum = jnp.concatenate([up_sum, rest_sum[0]], axis=1)
    out_sum = rest_sum[1]

    do_heads = exchange(do.reshape(g, hl, dh, t))
    first = jnp.full((1,), lax.axis_index("rep") * g if r > 1 else 0, jnp.int32)
    carried = attention_backward(qkv, kv, do_heads, o, lse, first)
    dqkv_heads = attention_backward(qkv, kv, do_heads, o, lse, first, carried)
    if r > 1:
        dqkv_heads = lax.psum_scatter(dqkv_heads, "rep", scatter_dimension=0, tiled=True)
    back = exchange(dqkv_heads).reshape(HEADS, 3, dh, t)
    head_grads = head_products(dqkv_heads, h1_all)
    head_grads = head_grads.transpose(1, 0, 2).reshape(devices, width, hl, 3 * dh)
    head_grads, back = lax.optimization_barrier((head_grads, back))
    head_grads = lax.all_to_all(head_grads, MESH_AXES, 0, 0, tiled=True)
    head_grads = head_grads.reshape(-1, r, g, width, hl, 3, dh).astype(F32)
    qkv_sum = jnp.sum(head_grads, axis=(0, 1))
    qkv_sum = qkv_sum.transpose(1, 3, 0, 2, 4).reshape(width, 3 * d)
    input_grad, small_one = finish(back, w_qkv, x, row(ln1_gain), row(ln1_bias), grad_middle)
    small = jnp.concatenate([small_one, small_two])
    small = small.reshape(4, devices, -1).transpose(1, 0, 2)
    small = jnp.sum(lax.all_to_all(small, MESH_AXES, 0, 0, tiled=True), axis=0)
    return (
        output[None], input_grad[None], small[0], small[1], qkv_sum, out_sum, small[2], small[3],
        up_sum, down_sum,
    )


def solution(mesh):
    n = mesh.shape["seq"]
    g = math.gcd(n, HEADS)
    shape = (mesh.shape["batch"], n // g, g // 4, 2, 2)
    fine = jax.sharding.Mesh(mesh.devices.reshape(shape), MESH_AXES)
    split = P("batch", SEQ, None)
    return jax.shard_map(
        body,
        mesh=fine,
        in_specs=(split, P(), P(), P(), P(), P(), P(), P(), P(), split),
        out_specs=(
            split,
            split,
            P(MESH_AXES),
            P(MESH_AXES),
            P(MESH_AXES, None),
            P(MESH_AXES, None),
            P(MESH_AXES),
            P(MESH_AXES),
            P(MESH_AXES, None),
            P(MESH_AXES, None),
        ),
        check_vma=False,
    )
```
